512 devices in a mesh: row: 16 (over z, core), col: 32 (over x, y).
Axes of the slice: x: 4, y: 8, z: 8, core: 2. Of those that a mesh axis runs over, the one named last changes fastest.
Arguments:
- panels: float32 [8192, 16384], P('row', 'col'), as said below
Outputs:
- r_rows: float32 [256, 16384], P(None, 'col')
Inputs may be any that keep to these rules, and one draw needn't show every extreme that they name: `panels`: the first 256 columns of W have full column rank.
All inputs are finite; a program needn't handle non-finite values.
Results may differ from the reference program's by a relative error of at most 0.0003.
Values sent between devices are 32-bit elements; how exact they have to be, the bound alone decides.
A program may use at most 64 MiB of HBM per device.

```python
import math
import jax
import jax.numpy as jnp
from jax import lax

PANEL = 128
COLBLK_DEV = 4
NROWS = 8192
NCOLS = 16384
N_COL = 32


def draw_panels(key, part):
    key_list = jax.random.split(jax.random.fold_in(key, 17), 4)
    local_width = COLBLK_DEV * PANEL
    position = jnp.arange(NROWS, dtype=jnp.float32) / max(NROWS - 1, 1)
    stored_col = jnp.arange(NCOLS, dtype=jnp.int32)
    is_panel = (stored_col < PANEL) | (stored_col >= local_width) & (stored_col < local_width + PANEL)
    row_scale = (1.0 + 2.0 * position) * jnp.exp(jax.random.uniform(key_list[0], (NROWS,), jnp.float32, 0.0, math.log(3.2)))
    col_unit = jax.random.uniform(key_list[1], (NCOLS,), jnp.float32, 0.0, 1.0)
    col_scale = 0.3 * jnp.exp(col_unit * math.log(10.0))
    noise_field = jax.random.truncated_normal(key_list[2], -4.0, 4.0, (NROWS, NCOLS), jnp.float32)
    base_field = noise_field * row_scale[:, None] * col_scale[None, :] * (0.25 / math.sqrt(NROWS))
    lead_cols = jnp.concatenate([base_field[:, 0:PANEL], base_field[:, local_width:local_width + PANEL]], axis=1)
    mixing = jax.random.normal(key_list[3], (2 * PANEL, NCOLS), jnp.float32) * (1.0 / math.sqrt(2 * PANEL))
    mixing = jnp.where(is_panel[None, :], 0.0, mixing)
    return base_field + jnp.dot(lead_cols, mixing, precision=lax.Precision.HIGHEST, preferred_element_type=jnp.float32)


def setup_inputs(seed: int = 0) -> dict:
    seeds = jax.random.split(jax.random.key(seed), 2)
    return {
        "panels": draw_panels(jax.random.fold_in(seeds[1], 71), 0),
    }


def product(left, right):
    return jnp.dot(left.astype(jnp.float32), right.astype(jnp.float32), precision=lax.Precision.HIGHEST, preferred_element_type=jnp.float32)

def reference(panels):
    local_width = COLBLK_DEV * PANEL
    lead_cols = jnp.concatenate([panels[:, 0:PANEL], panels[:, local_width:local_width + PANEL]], axis=1)
    lead_t = lead_cols.T
    first_low = jnp.linalg.cholesky(product(lead_t, lead_cols))
    basis_one = jax.scipy.linalg.solve_triangular(first_low, lead_t, lower=True)
    second_low = jnp.linalg.cholesky(product(basis_one, basis_one.T))
    cross_terms = product(lead_t, panels)
    half_solved = jax.scipy.linalg.solve_triangular(first_low, cross_terms, lower=True)
    top_block = jax.scipy.linalg.solve_triangular(second_low, half_solved, lower=True)
    stored_col = jnp.arange(NCOLS, dtype=jnp.int32)
    owner_col = stored_col // local_width
    within_col = stored_col % local_width
    global_col = (within_col // PANEL * N_COL + owner_col) * PANEL + within_col % PANEL
    row_iota = jnp.arange(2 * PANEL, dtype=jnp.int32)
    keep_mask = global_col[None, :] >= row_iota[:, None]
    return jnp.where(keep_mask, top_block, jnp.zeros_like(top_block))
```

```python
import jax
import jax.numpy as jnp
from jax import lax
from jax.experimental import pallas as pl
from jax.experimental.pallas import tpu as pltpu
from jax.sharding import PartitionSpec as P

PANEL = 128
LEAD = 2 * PANEL
LEAF = 64
SUB = 8
HI = lax.Precision.HIGHEST


def dot(left, right, dims):
    return lax.dot_general(left, right, (dims, ((), ())), precision=HI, preferred_element_type=jnp.float32)


NN = ((1,), (0,))
NT = ((1,), (1,))
TN = ((0,), (0,))


def leaf_inverse(block):
    groups = LEAF // SUB
    sub = lax.broadcasted_iota(jnp.int32, (SUB, 128), 0)

    def step(g, rows):
        rows = list(rows)
        live = [None] + [(q < groups - g) for q in range(1, groups)]
        cols = [[jnp.broadcast_to(rows[q][:, i:i + 1], (SUB, 128)) for i in range(SUB)] for q in range(groups)]
        pivots = jnp.ones((SUB, 128), jnp.float32)
        for i in range(SUB):
            pivots = jnp.where(sub == i, cols[0][i], pivots)
            inv = 1.0 / jnp.broadcast_to(cols[0][i][i:i + 1], (SUB, 128))
            line = jnp.broadcast_to(rows[0][i:i + 1], (SUB, 128)) * inv
            heads = [None] * SUB
            for j in range(i + 1, SUB):
                heads[j] = jnp.broadcast_to(cols[0][j][i:i + 1], (SUB, 128)) * inv
            for q in range(groups):
                keep = sub > i if q == 0 else live[q]
                mult = jnp.where(keep, cols[q][i], 0.0)
                rows[q] = rows[q] - mult * line
                for j in range(i + 1, SUB):
                    cols[q][j] = cols[q][j] - mult * heads[j]
        scale = lax.rsqrt(pivots)
        scale = scale * (1.5 - 0.5 * pivots * scale * scale)
        rows[0] = rows[0] * scale
        rows = rows[1:] + rows[:1]
        return tuple(pltpu.roll(r, 128 - SUB, 1) for r in rows)

    rows = tuple(block[q * SUB:(q + 1) * SUB] for q in range(groups))
    rows = lax.fori_loop(0, groups, step, rows)
    return jnp.concatenate(rows, axis=0)[:, :LEAF]


def chol_inverse(gram_ref, inv_ref, leaf_ref):
    inv_ref[...] = jnp.zeros_like(inv_ref)
    for b in range(LEAD // LEAF):
        at = pl.ds(b * LEAF, LEAF)
        strip = gram_ref[at, :]
        r = lax.broadcasted_iota(jnp.int32, (LEAF, LEAD), 0)
        c = lax.broadcasted_iota(jnp.int32, (LEAF, LEAD), 1)
        unit = jnp.where(c == r + b * LEAF, 1.0, 0.0).astype(jnp.float32)
        schur = dot(strip, unit, NT)
        rest = unit
        if b:
            done = inv_ref[...]
            low = dot(strip, done, NT)
            schur = schur - dot(low, low, NT)
            rest = unit - dot(low, done, NN)
        r = lax.broadcasted_iota(jnp.int32, (LEAF, 2 * LEAF), 0)
        c = lax.broadcasted_iota(jnp.int32, (LEAF, 2 * LEAF), 1)
        leaf_ref[...] = jnp.where(c == r + LEAF, 1.0, 0.0).astype(jnp.float32)
        leaf_ref[:, :LEAF] = schur
        leaf = leaf_inverse(leaf_ref[...])
        inv_ref[at, :] = dot(leaf, rest, NN)


def chol_inv_call(gram):
    return pl.pallas_call(
        chol_inverse,
        out_shape=jax.ShapeDtypeStruct((LEAD, LEAD), jnp.float32),
        scratch_shapes=[pltpu.VMEM((LEAF, 2 * LEAF), jnp.float32)],
    )(gram)


def local(panels):
    me = lax.axis_index("col")
    head = panels[:, :PANEL]
    zero = jnp.zeros_like(head)
    lead = lax.psum(
        jnp.concatenate([jnp.where(me == 0, head, zero), jnp.where(me == 1, head, zero)], axis=1), "col")
    gram = lax.psum(dot(lead, lead, TN), "row")
    cross = lax.psum(dot(lead, panels, TN), "row")
    inv_one = chol_inv_call(gram)
    basis = dot(inv_one, lead, NT)
    inv_two = chol_inv_call(lax.psum(dot(basis, basis, NT), "row"))
    top = dot(inv_two, dot(inv_one, cross, NN), NN)
    col_iota = jnp.arange(panels.shape[1], dtype=jnp.int32)
    global_col = (col_iota // PANEL * lax.axis_size("col") + me) * PANEL + col_iota % PANEL
    row_iota = jnp.arange(LEAD, dtype=jnp.int32)
    return jnp.where(global_col[None, :] >= row_iota[:, None], top, jnp.zeros_like(top))


def solution(mesh):
    return jax.shard_map(local, mesh=mesh, in_specs=(P("row", "col"),), out_specs=P(None, "col"), check_vma=False)
```

```python
import jax
import jax.numpy as jnp
from jax import lax
from jax.experimental import pallas as pl
from jax.experimental.pallas import tpu as pltpu
from jax.sharding import PartitionSpec as P

PANEL = 128
LEAD = 2 * PANEL
LEAF = 64
X_SIZE = 4
Y_SIZE = 8
N_ROW = 16
N_Z = 8
CHUNKS = 4
MESH = pl.DeviceIdType.MESH
SUB = 8
HI = lax.Precision.HIGHEST


def dot(left, right, dims):
    return lax.dot_general(left, right, (dims, ((), ())), precision=HI, preferred_element_type=jnp.float32)


NN = ((1,), (0,))
NT = ((1,), (1,))
TN = ((0,), (0,))


def leaf_inverse(block):
    groups = LEAF // SUB
    sub = lax.broadcasted_iota(jnp.int32, (SUB, 128), 0)

    def step(g, rows):
        rows = list(rows)
        live = [None] + [(q < groups - g) for q in range(1, groups)]
        cols = [[jnp.broadcast_to(rows[q][:, i:i + 1], (SUB, 128)) for i in range(SUB)] for q in range(groups)]
        pivots = jnp.ones((SUB, 128), jnp.float32)
        for i in range(SUB):
            pivots = jnp.where(sub == i, cols[0][i], pivots)
            inv = 1.0 / jnp.broadcast_to(cols[0][i][i:i + 1], (SUB, 128))
            line = jnp.broadcast_to(rows[0][i:i + 1], (SUB, 128)) * inv
            heads = [None] * SUB
            for j in range(i + 1, SUB):
                heads[j] = jnp.broadcast_to(cols[0][j][i:i + 1], (SUB, 128)) * inv
            for q in range(groups):
                keep = sub > i if q == 0 else live[q]
                mult = jnp.where(keep, cols[q][i], 0.0)
                rows[q] = rows[q] - mult * line
                for j in range(i + 1, SUB):
                    cols[q][j] = cols[q][j] - mult * heads[j]
        scale = lax.rsqrt(pivots)
        scale = scale * (1.5 - 0.5 * pivots * scale * scale)
        rows[0] = rows[0] * scale
        rows = rows[1:] + rows[:1]
        return tuple(pltpu.roll(r, 128 - SUB, 1) for r in rows)

    rows = tuple(block[q * SUB:(q + 1) * SUB] for q in range(groups))
    rows = lax.fori_loop(0, groups, step, rows)
    return jnp.concatenate(rows, axis=0)[:, :LEAF]


def chol_inverse(gram_ref, inv_ref, leaf_ref, between=()):
    inv_ref[...] = jnp.zeros(inv_ref.shape, jnp.float32)
    for b in range(LEAD // LEAF):
        at = pl.ds(b * LEAF, LEAF)
        strip = gram_ref[at, :]
        r = lax.broadcasted_iota(jnp.int32, (LEAF, LEAD), 0)
        c = lax.broadcasted_iota(jnp.int32, (LEAF, LEAD), 1)
        unit = jnp.where(c == r + b * LEAF, 1.0, 0.0).astype(jnp.float32)
        schur = dot(strip, unit, NT)
        rest = unit
        if b:
            done = inv_ref[...]
            low = dot(strip, done, NT)
            schur = schur - dot(low, low, NT)
            rest = unit - dot(low, done, NN)
        r = lax.broadcasted_iota(jnp.int32, (LEAF, 2 * LEAF), 0)
        c = lax.broadcasted_iota(jnp.int32, (LEAF, 2 * LEAF), 1)
        leaf_ref[...] = jnp.where(c == r + LEAF, 1.0, 0.0).astype(jnp.float32)
        leaf_ref[:, :LEAF] = schur
        leaf = leaf_inverse(leaf_ref[...])
        inv_ref[at, :] = dot(leaf, rest, NN)
        if b < len(between):
            between[b]()


def far_first(count):
    return sorted(range(1, count), key=lambda off: -min(off, count - off))


def kernel(panels_ref, out_ref, lead_ref, part_ref, recv_ref, gram_ref, inv_ref, leaf_ref,
           c_part, c_pair, c_half, c_recv, cross_ref,
           bc_send, bc_recv, rs_send, rs_recv, ag_send, ag_recv,
           pair_send, pair_recv, crs_send, crs_recv, cag_send, cag_recv):
    me = lax.axis_index("row")
    col = lax.axis_index("col")
    core = lax.rem(me, 2)
    z = me // 2
    x = col // Y_SIZE
    y = lax.rem(col, Y_SIZE)

    def at_xy(dx, dy):
        return {"col": lax.rem(x + dx + X_SIZE, X_SIZE) * Y_SIZE + lax.rem(y + dy + Y_SIZE, Y_SIZE)}

    def row_peer(off):
        return {"row": lax.rem(me + off, N_ROW)}

    partner = {"row": z * 2 + 1 - core}
    near = [at_xy(0, 1), at_xy(0, -1), at_xy(1, 0), at_xy(-1, 0)]

    barrier = pltpu.get_barrier_semaphore()
    for off in far_first(N_ROW):
        pl.semaphore_signal(barrier, inc=1, device_id=row_peer(off), device_id_type=MESH)
    for device in near:
        pl.semaphore_signal(barrier, inc=1, device_id=device, device_id_type=MESH)
    pl.semaphore_wait(barrier, N_ROW - 1 + len(near))

    half_rows = lead_ref.shape[1] // 2
    size = half_rows // CHUNKS

    def sends(tree, panel):
        d = lax.rem(y - panel + Y_SIZE, Y_SIZE)
        up, down = d <= 3, (d == 0) | (d >= 6)
        if tree == 0:
            return [(x == 0) & up, (x == 0) & down, x <= 1, x == 0]
        return [(x != 0) & up, (x != 0) & down, (d == 0) & (x <= 1),
                ((d == 0) & (x == 0)) | ((d != 0) & (x == 1))]

    def hop(k, tree, panel, way, own):
        rows = pl.ds(pl.multiple_of(tree * half_rows + k * size, size), size)
        piece = (k * 2 + tree) * 2 + panel
        return pltpu.make_async_remote_copy(
            src_ref=panels_ref.at[rows, pl.ds(0, PANEL)] if own else lead_ref.at[panel, rows],
            dst_ref=lead_ref.at[panel, rows],
            send_sem=bc_send.at[piece, way], recv_sem=bc_recv.at[piece],
            device_id=near[way], device_id_type=MESH)

    def pass_on(k, carry):
        for tree in range(2):
            for panel in range(2):
                cond = sends(tree, panel)

                @pl.when(col == panel)
                def _():
                    for way in range(4):
                        @pl.when(cond[way])
                        def _():
                            hop(k, tree, panel, way, True).start()

                @pl.when(col != panel)
                def _():
                    hop(k, tree, panel, 0, False).wait_recv()
                    for way in range(4):
                        @pl.when(cond[way])
                        def _():
                            hop(k, tree, panel, way, False).start()
        return carry

    lax.fori_loop(0, CHUNKS, pass_on, 0)
    for panel in range(2):
        @pl.when(col == panel)
        def _():
            lead_ref[panel] = panels_ref[:, :PANEL]

    def lead():
        return jnp.concatenate([lead_ref[0], lead_ref[1]], axis=1)

    own_rows = N_ROW
    mine = pl.ds(pl.multiple_of(me * own_rows, own_rows), own_rows)

    def rs_copy(p, off):
        peer = lax.rem(me + off, N_ROW)
        return pltpu.make_async_remote_copy(
            src_ref=part_ref.at[p, pl.ds(pl.multiple_of(peer * own_rows, own_rows), own_rows)],
            dst_ref=recv_ref.at[p, off - 1],
            send_sem=rs_send.at[p, off - 1], recv_sem=rs_recv.at[p, off - 1],
            device_id=row_peer(off), device_id_type=MESH)

    def ag_copy(p, off):
        return pltpu.make_async_remote_copy(
            src_ref=gram_ref.at[p, mine], dst_ref=gram_ref.at[p, mine],
            send_sem=ag_send.at[p, off - 1], recv_sem=ag_recv.at[p, off - 1],
            device_id=row_peer(off), device_id_type=MESH)

    def scatter_start(p):
        for off in far_first(N_ROW):
            rs_copy(p, off).start()

    def scatter_finish(p):
        total = part_ref[p, mine]
        for off in reversed(far_first(N_ROW)):
            rs_copy(p, off).wait_recv()
            total = total + recv_ref[p, off - 1]
        gram_ref[p, mine] = total
        for off in far_first(N_ROW):
            ag_copy(p, off).start()

    def gather_finish(p):
        for off in reversed(far_first(N_ROW)):
            ag_copy(p, off).wait_recv()

    c_rows = LEAD // 2 // N_Z
    keep = pl.ds(pl.multiple_of(core * PANEL, PANEL), PANEL)
    give = pl.ds(pl.multiple_of((1 - core) * PANEL, PANEL), PANEL)
    c_mine = pl.ds(pl.multiple_of(core * PANEL + z * c_rows, c_rows), c_rows)

    def pair_copy(step):
        return pltpu.make_async_remote_copy(
            src_ref=cross_ref.at[keep] if step else c_part.at[give],
            dst_ref=cross_ref.at[keep] if step else c_pair,
            send_sem=pair_send.at[step], recv_sem=pair_recv.at[step],
            device_id=partner, device_id_type=MESH)

    def crs_copy(off):
        peer_z = lax.rem(z + off, N_Z)
        return pltpu.make_async_remote_copy(
            src_ref=c_half.at[pl.ds(pl.multiple_of(peer_z * c_rows, c_rows), c_rows)],
            dst_ref=c_recv.at[off - 1],
            send_sem=crs_send.at[off - 1], recv_sem=crs_recv.at[off - 1],
            device_id=row_peer(2 * off), device_id_type=MESH)

    def cag_copy(off):
        return pltpu.make_async_remote_copy(
            src_ref=cross_ref.at[c_mine], dst_ref=cross_ref.at[c_mine],
            send_sem=cag_send.at[off - 1], recv_sem=cag_recv.at[off - 1],
            device_id=row_peer(2 * off), device_id_type=MESH)

    def cross_scatter():
        pair_copy(0).wait_recv()
        c_half[...] = c_part[keep] + c_pair[...]
        for off in far_first(N_Z):
            crs_copy(off).start()

    def cross_gather():
        total = c_half[pl.ds(pl.multiple_of(z * c_rows, c_rows), c_rows)]
        for off in reversed(far_first(N_Z)):
            crs_copy(off).wait_recv()
            total = total + c_recv[off - 1]
        cross_ref[c_mine] = total
        for off in far_first(N_Z):
            cag_copy(off).start()

    def cross_pair():
        for off in far_first(N_Z):
            cag_copy(off).wait_recv()
        pair_copy(1).start()

    part_ref[0] = dot(lead(), lead(), TN)
    scatter_start(0)
    c_part[...] = dot(lead(), panels_ref[...], TN)
    pair_copy(0).start()
    scatter_finish(0)
    gather_finish(0)
    cross_scatter()
    chol_inverse(gram_ref.at[0], inv_ref.at[0], leaf_ref, (lambda: None, cross_gather))
    basis = dot(inv_ref[0], lead(), NT)
    part_ref[1] = dot(basis, basis, NT)
    scatter_start(1)
    cross_pair()
    scatter_finish(1)
    pair_copy(1).wait_recv()
    c_part_done = [pair_copy(0), pair_copy(1)]
    for copy in c_part_done:
        copy.wait_send()
    c_part[...] = dot(inv_ref[0], cross_ref[...], NN)
    gather_finish(1)
    chol_inverse(gram_ref.at[1], inv_ref.at[1], leaf_ref)
    top = dot(inv_ref[1], c_part[...], NN)
    width = out_ref.shape[1]
    r = lax.broadcasted_iota(jnp.int32, (LEAD, width), 0)
    c = lax.broadcasted_iota(jnp.int32, (LEAD, width), 1)
    global_col = (c // PANEL * (X_SIZE * Y_SIZE) + col) * PANEL + lax.rem(c, PANEL)
    out_ref[...] = jnp.where(global_col >= r, top, 0.0)

    for p in range(2):
        for off in range(1, N_ROW):
            rs_copy(p, off).wait_send()
            ag_copy(p, off).wait_send()
    for off in range(1, N_Z):
        crs_copy(off).wait_send()
        cag_copy(off).wait_send()

    def drain(k, carry):
        for tree in range(2):
            for panel in range(2):
                cond = sends(tree, panel)
                for way in range(4):
                    @pl.when(cond[way])
                    def _():
                        hop(k, tree, panel, way, False).wait_send()
        return carry

    lax.fori_loop(0, CHUNKS, drain, 0)


def local(panels):
    rows, width = panels.shape
    f32 = jnp.float32
    vmem, dma = pltpu.VMEM, pltpu.SemaphoreType.DMA
    return pl.pallas_call(
        kernel,
        out_shape=jax.ShapeDtypeStruct((LEAD, width), f32),
        in_specs=[pl.BlockSpec(memory_space=vmem)],
        out_specs=pl.BlockSpec(memory_space=vmem),
        scratch_shapes=[
            vmem((2, rows, PANEL), f32),
            vmem((2, LEAD, LEAD), f32),
            vmem((2, N_ROW - 1, N_ROW, LEAD), f32),
            vmem((2, LEAD, LEAD), f32),
            vmem((2, LEAD, LEAD), f32),
            vmem((LEAF, 2 * LEAF), f32),
            vmem((LEAD, width), f32),
            vmem((PANEL, width), f32),
            vmem((PANEL, width), f32),
            vmem((N_Z - 1, LEAD // 2 // N_Z, width), f32),
            vmem((LEAD, width), f32),
            dma((CHUNKS * 4, 4)), dma((CHUNKS * 4,)),
            dma((2, N_ROW - 1)), dma((2, N_ROW - 1)),
            dma((2, N_ROW - 1)), dma((2, N_ROW - 1)),
            dma((2,)), dma((2,)),
            dma((N_Z - 1,)), dma((N_Z - 1,)),
            dma((N_Z - 1,)), dma((N_Z - 1,)),
        ],
        compiler_params=pltpu.CompilerParams(collective_id=0, has_side_effects=True),
    )(panels)


def solution(mesh):
    return jax.shard_map(local, mesh=mesh, in_specs=(P("row", "col"),), out_specs=P(None, "col"), check_vma=False)
```

```python
import jax
import jax.numpy as jnp
from jax import lax
from jax.experimental import pallas as pl
from jax.experimental.pallas import tpu as pltpu
from jax.sharding import PartitionSpec as P

PANEL = 128
LEAD = 2 * PANEL
LEAF = 64
X_SIZE = 4
Y_SIZE = 8
N_ROW = 16
N_Z = 8
CHUNKS = 4
MESH = pl.DeviceIdType.MESH
SUB = 8
HI = lax.Precision.HIGHEST


def dot(left, right, dims):
    return lax.dot_general(left, right, (dims, ((), ())), precision=HI, preferred_element_type=jnp.float32)


NN = ((1,), (0,))
NT = ((1,), (1,))
TN = ((0,), (0,))


def leaf_inverse(block):
    groups = LEAF // SUB
    sub = lax.broadcasted_iota(jnp.int32, (SUB, 128), 0)

    def step(g, rows):
        rows = list(rows)
        live = [None] + [(q < groups - g) for q in range(1, groups)]
        cols = [[jnp.broadcast_to(rows[q][:, i:i + 1], (SUB, 128)) for i in range(SUB)] for q in range(groups)]
        pivots = jnp.ones((SUB, 128), jnp.float32)
        for i in range(SUB):
            pivots = jnp.where(sub == i, cols[0][i], pivots)
            inv = 1.0 / jnp.broadcast_to(cols[0][i][i:i + 1], (SUB, 128))
            line = jnp.broadcast_to(rows[0][i:i + 1], (SUB, 128)) * inv
            heads = [None] * SUB
            for j in range(i + 1, SUB):
                heads[j] = jnp.broadcast_to(cols[0][j][i:i + 1], (SUB, 128)) * inv
            for q in range(groups):
                keep = sub > i if q == 0 else live[q]
                mult = jnp.where(keep, cols[q][i], 0.0)
                rows[q] = rows[q] - mult * line
                for j in range(i + 1, SUB):
                    cols[q][j] = cols[q][j] - mult * heads[j]
        scale = lax.rsqrt(pivots)
        scale = scale * (1.5 - 0.5 * pivots * scale * scale)
        rows[0] = rows[0] * scale
        rows = rows[1:] + rows[:1]
        return tuple(pltpu.roll(r, 128 - SUB, 1) for r in rows)

    rows = tuple(block[q * SUB:(q + 1) * SUB] for q in range(groups))
    rows = lax.fori_loop(0, groups, step, rows)
    return jnp.concatenate(rows, axis=0)[:, :LEAF]


def chol_inverse(gram_ref, inv_ref, leaf_ref, between=()):
    inv_ref[...] = jnp.zeros(inv_ref.shape, jnp.float32)
    for b in range(LEAD // LEAF):
        at = pl.ds(b * LEAF, LEAF)
        strip = gram_ref[at, :]
        r = lax.broadcasted_iota(jnp.int32, (LEAF, LEAD), 0)
        c = lax.broadcasted_iota(jnp.int32, (LEAF, LEAD), 1)
        unit = jnp.where(c == r + b * LEAF, 1.0, 0.0).astype(jnp.float32)
        schur = dot(strip, unit, NT)
        rest = unit
        if b:
            done = inv_ref[...]
            low = dot(strip, done, NT)
            schur = schur - dot(low, low, NT)
            rest = unit - dot(low, done, NN)
        r = lax.broadcasted_iota(jnp.int32, (LEAF, 2 * LEAF), 0)
        c = lax.broadcasted_iota(jnp.int32, (LEAF, 2 * LEAF), 1)
        leaf_ref[...] = jnp.where(c == r + LEAF, 1.0, 0.0).astype(jnp.float32)
        leaf_ref[:, :LEAF] = schur
        leaf = leaf_inverse(leaf_ref[...])
        inv_ref[at, :] = dot(leaf, rest, NN)
        if b < len(between):
            between[b]()


def far_first(count):
    return sorted(range(1, count), key=lambda off: -min(off, count - off))


def kernel(panels_ref, out_ref, lead_ref, part_ref, recv_ref, gram_ref, inv_ref, leaf_ref,
           c_part, c_pair, c_half, c_recv, cross_ref,
           bc_send, bc_recv, rs_send, rs_recv, ag_send, ag_recv,
           pair_send, pair_recv, crs_send, crs_recv, cag_send, cag_recv):
    me = lax.axis_index("row")
    col = lax.axis_index("col")
    core = lax.rem(me, 2)
    z = me // 2
    x = col // Y_SIZE
    y = lax.rem(col, Y_SIZE)

    def at_xy(dx, dy):
        return {"col": lax.rem(x + dx + X_SIZE, X_SIZE) * Y_SIZE + lax.rem(y + dy + Y_SIZE, Y_SIZE)}

    def row_peer(off):
        return {"row": lax.rem(me + off, N_ROW)}

    partner = {"row": z * 2 + 1 - core}
    near = [at_xy(0, 1), at_xy(0, -1), at_xy(1, 0), at_xy(-1, 0)]

    barrier = pltpu.get_barrier_semaphore()
    for off in far_first(N_ROW):
        pl.semaphore_signal(barrier, inc=1, device_id=row_peer(off), device_id_type=MESH)
    for device in near:
        pl.semaphore_signal(barrier, inc=1, device_id=device, device_id_type=MESH)
    pl.semaphore_wait(barrier, N_ROW - 1 + len(near))

    half_rows = lead_ref.shape[1] // 2
    size = half_rows // CHUNKS

    def sends(tree, panel):
        d = lax.rem(y - panel + Y_SIZE, Y_SIZE)
        up, down = d <= 3, (d == 0) | (d >= 6)
        if tree == 0:
            return [(x == 0) & up, (x == 0) & down, x <= 1, x == 0]
        return [(x != 0) & up, (x != 0) & down, (d == 0) & (x <= 1),
                ((d == 0) & (x == 0)) | ((d != 0) & (x == 1))]

    def relays(cond):
        return cond[0] | cond[1] | cond[2] | cond[3]

    def hop(k, tree, panel, way, own):
        rows = pl.ds(pl.multiple_of(tree * half_rows + k * size, size), size)
        piece = (k * 2 + tree) * 2 + panel
        return pltpu.make_async_remote_copy(
            src_ref=panels_ref.at[rows, pl.ds(0, PANEL)] if own else lead_ref.at[panel, rows],
            dst_ref=lead_ref.at[panel, rows],
            send_sem=bc_send.at[piece, way], recv_sem=bc_recv.at[piece],
            device_id=near[way], device_id_type=MESH)

    def pass_on(k, carry):
        for tree in range(2):
            for panel in range(2):
                cond = sends(tree, panel)

                @pl.when(col == panel)
                def _():
                    for way in range(4):
                        @pl.when(cond[way])
                        def _():
                            hop(k, tree, panel, way, True).start()

                @pl.when((col != panel) & relays(cond))
                def _():
                    hop(k, tree, panel, 0, False).wait_recv()
                    for way in range(4):
                        @pl.when(cond[way])
                        def _():
                            hop(k, tree, panel, way, False).start()
        return carry

    def take_last(k, carry):
        for tree in range(2):
            for panel in range(2):
                @pl.when((col != panel) & jnp.logical_not(relays(sends(tree, panel))))
                def _():
                    hop(k, tree, panel, 0, False).wait_recv()
        return carry

    lax.fori_loop(0, CHUNKS, pass_on, 0)
    lax.fori_loop(0, CHUNKS, take_last, 0)
    for panel in range(2):
        @pl.when(col == panel)
        def _():
            lead_ref[panel] = panels_ref[:, :PANEL]

    def lead():
        return jnp.concatenate([lead_ref[0], lead_ref[1]], axis=1)

    own_rows = N_ROW
    mine = pl.ds(pl.multiple_of(me * own_rows, own_rows), own_rows)

    def rs_copy(p, off):
        peer = lax.rem(me + off, N_ROW)
        return pltpu.make_async_remote_copy(
            src_ref=part_ref.at[p, pl.ds(pl.multiple_of(peer * own_rows, own_rows), own_rows)],
            dst_ref=recv_ref.at[p, off - 1],
            send_sem=rs_send.at[p, off - 1], recv_sem=rs_recv.at[p, off - 1],
            device_id=row_peer(off), device_id_type=MESH)

    def ag_copy(p, off):
        return pltpu.make_async_remote_copy(
            src_ref=gram_ref.at[p, mine], dst_ref=gram_ref.at[p, mine],
            send_sem=ag_send.at[p, off - 1], recv_sem=ag_recv.at[p, off - 1],
            device_id=row_peer(off), device_id_type=MESH)

    def scatter_start(p):
        for off in far_first(N_ROW):
            rs_copy(p, off).start()

    def scatter_finish(p):
        total = part_ref[p, mine]
        for off in reversed(far_first(N_ROW)):
            rs_copy(p, off).wait_recv()
            total = total + recv_ref[p, off - 1]
        gram_ref[p, mine] = total
        for off in far_first(N_ROW):
            ag_copy(p, off).start()

    def gather_finish(p):
        for off in reversed(far_first(N_ROW)):
            ag_copy(p, off).wait_recv()

    c_rows = LEAD // 2 // N_Z
    keep = pl.ds(pl.multiple_of(core * PANEL, PANEL), PANEL)
    give = pl.ds(pl.multiple_of((1 - core) * PANEL, PANEL), PANEL)
    c_mine = pl.ds(pl.multiple_of(core * PANEL + z * c_rows, c_rows), c_rows)

    def pair_copy(step):
        return pltpu.make_async_remote_copy(
            src_ref=cross_ref.at[keep] if step else c_part.at[give],
            dst_ref=cross_ref.at[keep] if step else c_pair,
            send_sem=pair_send.at[step], recv_sem=pair_recv.at[step],
            device_id=partner, device_id_type=MESH)

    def crs_copy(off):
        peer_z = lax.rem(z + off, N_Z)
        return pltpu.make_async_remote_copy(
            src_ref=c_half.at[pl.ds(pl.multiple_of(peer_z * c_rows, c_rows), c_rows)],
            dst_ref=c_recv.at[off - 1],
            send_sem=crs_send.at[off - 1], recv_sem=crs_recv.at[off - 1],
            device_id=row_peer(2 * off), device_id_type=MESH)

    def cag_copy(off):
        return pltpu.make_async_remote_copy(
            src_ref=cross_ref.at[c_mine], dst_ref=cross_ref.at[c_mine],
            send_sem=cag_send.at[off - 1], recv_sem=cag_recv.at[off - 1],
            device_id=row_peer(2 * off), device_id_type=MESH)

    def cross_scatter():
        pair_copy(0).wait_recv()
        c_half[...] = c_part[keep] + c_pair[...]
        for off in far_first(N_Z):
            crs_copy(off).start()

    def cross_gather():
        total = c_half[pl.ds(pl.multiple_of(z * c_rows, c_rows), c_rows)]
        for off in reversed(far_first(N_Z)):
            crs_copy(off).wait_recv()
            total = total + c_recv[off - 1]
        cross_ref[c_mine] = total
        for off in far_first(N_Z):
            cag_copy(off).start()

    def cross_pair():
        for off in far_first(N_Z):
            cag_copy(off).wait_recv()
        pair_copy(1).start()

    part_ref[0] = dot(lead(), lead(), TN)
    scatter_start(0)
    c_part[...] = dot(lead(), panels_ref[...], TN)
    pair_copy(0).start()
    scatter_finish(0)
    gather_finish(0)
    cross_scatter()
    chol_inverse(gram_ref.at[0], inv_ref.at[0], leaf_ref, (lambda: None, cross_gather))
    basis = dot(inv_ref[0], lead(), NT)
    part_ref[1] = dot(basis, basis, NT)
    scatter_start(1)
    cross_pair()
    scatter_finish(1)
    pair_copy(1).wait_recv()
    c_part_done = [pair_copy(0), pair_copy(1)]
    for copy in c_part_done:
        copy.wait_send()
    c_part[...] = dot(inv_ref[0], cross_ref[...], NN)
    gather_finish(1)
    chol_inverse(gram_ref.at[1], inv_ref.at[1], leaf_ref)
    top = dot(inv_ref[1], c_part[...], NN)
    width = out_ref.shape[1]
    r = lax.broadcasted_iota(jnp.int32, (LEAD, width), 0)
    c = lax.broadcasted_iota(jnp.int32, (LEAD, width), 1)
    global_col = (c // PANEL * (X_SIZE * Y_SIZE) + col) * PANEL + lax.rem(c, PANEL)
    out_ref[...] = jnp.where(global_col >= r, top, 0.0)

    for p in range(2):
        for off in range(1, N_ROW):
            rs_copy(p, off).wait_send()
            ag_copy(p, off).wait_send()
    for off in range(1, N_Z):
        crs_copy(off).wait_send()
        cag_copy(off).wait_send()

    def drain(k, carry):
        for tree in range(2):
            for panel in range(2):
                cond = sends(tree, panel)
                for way in range(4):
                    @pl.when(cond[way])
                    def _():
                        hop(k, tree, panel, way, False).wait_send()
        return carry

    lax.fori_loop(0, CHUNKS, drain, 0)


def local(panels):
    rows, width = panels.shape
    f32 = jnp.float32
    vmem, dma = pltpu.VMEM, pltpu.SemaphoreType.DMA
    return pl.pallas_call(
        kernel,
        out_shape=jax.ShapeDtypeStruct((LEAD, width), f32),
        in_specs=[pl.BlockSpec(memory_space=vmem)],
        out_specs=pl.BlockSpec(memory_space=vmem),
        scratch_shapes=[
            vmem((2, rows, PANEL), f32),
            vmem((2, LEAD, LEAD), f32),
            vmem((2, N_ROW - 1, N_ROW, LEAD), f32),
            vmem((2, LEAD, LEAD), f32),
            vmem((2, LEAD, LEAD), f32),
            vmem((LEAF, 2 * LEAF), f32),
            vmem((LEAD, width), f32),
            vmem((PANEL, width), f32),
            vmem((PANEL, width), f32),
            vmem((N_Z - 1, LEAD // 2 // N_Z, width), f32),
            vmem((LEAD, width), f32),
            dma((CHUNKS * 4, 4)), dma((CHUNKS * 4,)),
            dma((2, N_ROW - 1)), dma((2, N_ROW - 1)),
            dma((2, N_ROW - 1)), dma((2, N_ROW - 1)),
            dma((2,)), dma((2,)),
            dma((N_Z - 1,)), dma((N_Z - 1,)),
            dma((N_Z - 1,)), dma((N_Z - 1,)),
        ],
        compiler_params=pltpu.CompilerParams(collective_id=0, has_side_effects=True),
    )(panels)


def solution(mesh):
    return jax.shard_map(local, mesh=mesh, in_specs=(P("row", "col"),), out_specs=P(None, "col"), check_vma=False)
```

```python
import jax
import jax.numpy as jnp
from jax import lax
from jax.experimental import pallas as pl
from jax.experimental.pallas import tpu as pltpu
from jax.sharding import PartitionSpec as P

PANEL = 128
LEAD = 2 * PANEL
LEAF = 64
X_SIZE = 4
Y_SIZE = 8
N_ROW = 16
N_Z = 8
CHUNKS = 2
MESH = pl.DeviceIdType.MESH
SUB = 8
HI = lax.Precision.HIGHEST


def dot(left, right, dims):
    return lax.dot_general(left, right, (dims, ((), ())), precision=HI, preferred_element_type=jnp.float32)


NN = ((1,), (0,))
NT = ((1,), (1,))
TN = ((0,), (0,))


def leaf_inverse(block):
    groups = LEAF // SUB
    sub = lax.broadcasted_iota(jnp.int32, (SUB, 128), 0)

    def step(g, rows):
        rows = list(rows)
        live = [None] + [(q < groups - g) for q in range(1, groups)]
        cols = [[jnp.broadcast_to(rows[q][:, i:i + 1], (SUB, 128)) for i in range(SUB)] for q in range(groups)]
        pivots = jnp.ones((SUB, 128), jnp.float32)
        for i in range(SUB):
            pivots = jnp.where(sub == i, cols[0][i], pivots)
            inv = 1.0 / jnp.broadcast_to(cols[0][i][i:i + 1], (SUB, 128))
            line = jnp.broadcast_to(rows[0][i:i + 1], (SUB, 128)) * inv
            heads = [None] * SUB
            for j in range(i + 1, SUB):
                heads[j] = jnp.broadcast_to(cols[0][j][i:i + 1], (SUB, 128)) * inv
            for q in range(groups):
                keep = sub > i if q == 0 else live[q]
                mult = jnp.where(keep, cols[q][i], 0.0)
                rows[q] = rows[q] - mult * line
                for j in range(i + 1, SUB):
                    cols[q][j] = cols[q][j] - mult * heads[j]
        scale = lax.rsqrt(pivots)
        scale = scale * (1.5 - 0.5 * pivots * scale * scale)
        rows[0] = rows[0] * scale
        rows = rows[1:] + rows[:1]
        return tuple(pltpu.roll(r, 128 - SUB, 1) for r in rows)

    rows = tuple(block[q * SUB:(q + 1) * SUB] for q in range(groups))
    rows = lax.fori_loop(0, groups, step, rows)
    rows = jnp.concatenate(rows, axis=0)
    return jnp.where(lax.broadcasted_iota(jnp.int32, rows.shape, 1) < LEAF, rows, 0.0)


def panel_inverse(block):
    r = lax.broadcasted_iota(jnp.int32, (LEAF, PANEL), 0)
    c = lax.broadcasted_iota(jnp.int32, (LEAF, PANEL), 1)
    unit = jnp.where(c == r + LEAF, 1.0, 0.0).astype(jnp.float32)
    none = jnp.zeros((LEAF, PANEL), jnp.float32)
    first = leaf_inverse(jnp.where(c < LEAF, block[:LEAF], unit))
    above = jnp.concatenate([first, none], axis=0)
    low = dot(block[LEAF:], above, NT)
    schur = block[LEAF:] - dot(low, jnp.concatenate([none, low], axis=0), NT)
    rest = unit - dot(low, above, NN)
    second = leaf_inverse(jnp.where(c < LEAF, pltpu.roll(schur, LEAF, 1), unit))
    return jnp.concatenate([first, dot(second, jnp.concatenate([rest, none], axis=0), NN)], axis=0)


def chol_inverse(gram_ref, inv_ref, between=lambda: None):
    first = panel_inverse(gram_ref[:PANEL, :PANEL])
    low = dot(gram_ref[PANEL:, :PANEL], first, NT)
    schur = gram_ref[PANEL:, PANEL:] - dot(low, low, NT)
    inv_ref[:PANEL, :PANEL] = first
    inv_ref[:PANEL, PANEL:] = jnp.zeros((PANEL, PANEL), jnp.float32)
    between()
    rest = dot(low, first, NN)
    second = panel_inverse(schur)
    inv_ref[PANEL:, PANEL:] = second
    inv_ref[PANEL:, :PANEL] = -dot(second, rest, NN)


def far_first(count):
    return sorted(range(1, count), key=lambda off: -min(off, count - off))


def kernel(panels_ref, out_ref, lead_ref, part_ref, recv_ref, gram_ref, inv_ref,
           c_part, c_pair, c_half, c_recv, cross_ref,
           bc_send, bc_recv, rs_send, rs_recv, ag_send, ag_recv,
           pair_send, pair_recv, crs_send, crs_recv, cag_send, cag_recv):
    me = lax.axis_index("row")
    col = lax.axis_index("col")
    core = lax.rem(me, 2)
    z = me // 2
    x = col // Y_SIZE
    y = lax.rem(col, Y_SIZE)

    def at_xy(dx, dy):
        return {"col": lax.rem(x + dx + X_SIZE, X_SIZE) * Y_SIZE + lax.rem(y + dy + Y_SIZE, Y_SIZE)}

    def row_peer(off):
        return {"row": lax.rem(me + off, N_ROW)}

    partner = {"row": z * 2 + 1 - core}
    near = [at_xy(0, 1), at_xy(0, -1), at_xy(1, 0), at_xy(-1, 0)]

    barrier = pltpu.get_barrier_semaphore()
    for off in far_first(N_ROW):
        pl.semaphore_signal(barrier, inc=1, device_id=row_peer(off), device_id_type=MESH)
    for device in near:
        pl.semaphore_signal(barrier, inc=1, device_id=device, device_id_type=MESH)
    pl.semaphore_wait(barrier, N_ROW - 1 + len(near))

    half_rows = lead_ref.shape[1] // 2
    size = half_rows // CHUNKS

    def sends(tree, panel):
        d = lax.rem(y - panel + Y_SIZE, Y_SIZE)
        up, down = d <= 3, (d == 0) | (d >= 6)
        if tree == 0:
            return [(x == 0) & up, (x == 0) & down, x <= 1, x == 0]
        return [(x != 0) & up, (x != 0) & down, (d == 0) & (x <= 1),
                ((d == 0) & (x == 0)) | ((d != 0) & (x == 1))]

    def relays(cond):
        return cond[0] | cond[1] | cond[2] | cond[3]

    def hop(k, tree, panel, way, own):
        rows = pl.ds(pl.multiple_of(tree * half_rows + k * size, size), size)
        piece = (k * 2 + tree) * 2 + panel
        return pltpu.make_async_remote_copy(
            src_ref=panels_ref.at[rows, pl.ds(0, PANEL)] if own else lead_ref.at[panel, rows],
            dst_ref=lead_ref.at[panel, rows],
            send_sem=bc_send.at[piece, way], recv_sem=bc_recv.at[piece],
            device_id=near[way], device_id_type=MESH)

    def send_own(k, carry):
        for panel in range(2):
            @pl.when(col == panel)
            def _():
                for tree in range(2):
                    cond = sends(tree, panel)
                    for way in range(4):
                        @pl.when(cond[way])
                        def _():
                            hop(k, tree, panel, way, True).start()
        return carry

    def pass_on(k, carry):
        for tree in range(2):
            for panel in range(2):
                cond = sends(tree, panel)

                @pl.when((col != panel) & relays(cond))
                def _():
                    hop(k, tree, panel, 0, False).wait_recv()
                    for way in range(4):
                        @pl.when(cond[way])
                        def _():
                            hop(k, tree, panel, way, False).start()
        return carry

    def take_last(k, carry):
        for tree in range(2):
            for panel in range(2):
                @pl.when((col != panel) & jnp.logical_not(relays(sends(tree, panel))))
                def _():
                    hop(k, tree, panel, 0, False).wait_recv()
        return carry

    lax.fori_loop(0, CHUNKS, send_own, 0)
    lax.fori_loop(0, CHUNKS, pass_on, 0)
    lax.fori_loop(0, CHUNKS, take_last, 0)
    for panel in range(2):
        @pl.when(col == panel)
        def _():
            lead_ref[panel] = panels_ref[:, :PANEL]

    def lead():
        return jnp.concatenate([lead_ref[0], lead_ref[1]], axis=1)

    own_rows = N_ROW
    mine = pl.ds(pl.multiple_of(me * own_rows, own_rows), own_rows)

    def rs_copy(p, off):
        peer = lax.rem(me + off, N_ROW)
        return pltpu.make_async_remote_copy(
            src_ref=part_ref.at[p, pl.ds(pl.multiple_of(peer * own_rows, own_rows), own_rows)],
            dst_ref=recv_ref.at[p, off - 1],
            send_sem=rs_send.at[p, off - 1], recv_sem=rs_recv.at[p, off - 1],
            device_id=row_peer(off), device_id_type=MESH)

    def ag_copy(p, off):
        return pltpu.make_async_remote_copy(
            src_ref=gram_ref.at[p, mine], dst_ref=gram_ref.at[p, mine],
            send_sem=ag_send.at[p, off - 1], recv_sem=ag_recv.at[p, off - 1],
            device_id=row_peer(off), device_id_type=MESH)

    def scatter_start(p):
        for off in far_first(N_ROW):
            rs_copy(p, off).start()

    def scatter_finish(p):
        total = part_ref[p, mine]
        for off in reversed(far_first(N_ROW)):
            rs_copy(p, off).wait_recv()
            total = total + recv_ref[p, off - 1]
        gram_ref[p, mine] = total
        for off in far_first(N_ROW):
            ag_copy(p, off).start()

    def gather_finish(p):
        for off in reversed(far_first(N_ROW)):
            ag_copy(p, off).wait_recv()

    c_rows = LEAD // 2 // N_Z
    keep = pl.ds(pl.multiple_of(core * PANEL, PANEL), PANEL)
    give = pl.ds(pl.multiple_of((1 - core) * PANEL, PANEL), PANEL)
    c_mine = pl.ds(pl.multiple_of(core * PANEL + z * c_rows, c_rows), c_rows)

    def pair_copy(step):
        return pltpu.make_async_remote_copy(
            src_ref=cross_ref.at[keep] if step else c_part.at[give],
            dst_ref=cross_ref.at[keep] if step else c_pair,
            send_sem=pair_send.at[step], recv_sem=pair_recv.at[step],
            device_id=partner, device_id_type=MESH)

    def crs_copy(off):
        peer_z = lax.rem(z + off, N_Z)
        return pltpu.make_async_remote_copy(
            src_ref=c_half.at[pl.ds(pl.multiple_of(peer_z * c_rows, c_rows), c_rows)],
            dst_ref=c_recv.at[off - 1],
            send_sem=crs_send.at[off - 1], recv_sem=crs_recv.at[off - 1],
            device_id=row_peer(2 * off), device_id_type=MESH)

    def cag_copy(off):
        return pltpu.make_async_remote_copy(
            src_ref=cross_ref.at[c_mine], dst_ref=cross_ref.at[c_mine],
            send_sem=cag_send.at[off - 1], recv_sem=cag_recv.at[off - 1],
            device_id=row_peer(2 * off), device_id_type=MESH)

    def cross_scatter():
        pair_copy(0).wait_recv()
        c_half[...] = c_part[keep] + c_pair[...]
        for off in far_first(N_Z):
            crs_copy(off).start()

    def cross_gather():
        total = c_half[pl.ds(pl.multiple_of(z * c_rows, c_rows), c_rows)]
        for off in reversed(far_first(N_Z)):
            crs_copy(off).wait_recv()
            total = total + c_recv[off - 1]
        cross_ref[c_mine] = total
        for off in far_first(N_Z):
            cag_copy(off).start()

    def cross_pair():
        for off in far_first(N_Z):
            cag_copy(off).wait_recv()
        pair_copy(1).start()

    part_ref[0] = dot(lead(), lead(), TN)
    scatter_start(0)
    c_part[...] = dot(lead(), panels_ref[...], TN)
    pair_copy(0).start()
    scatter_finish(0)
    gather_finish(0)
    cross_scatter()
    chol_inverse(gram_ref.at[0], inv_ref.at[0], cross_gather)
    basis = dot(inv_ref[0], lead(), NT)
    part_ref[1] = dot(basis, basis, NT)
    scatter_start(1)
    cross_pair()
    scatter_finish(1)
    pair_copy(1).wait_recv()
    c_part_done = [pair_copy(0), pair_copy(1)]
    for copy in c_part_done:
        copy.wait_send()
    c_part[...] = dot(inv_ref[0], cross_ref[...], NN)
    gather_finish(1)
    chol_inverse(gram_ref.at[1], inv_ref.at[1])
    top = dot(inv_ref[1], c_part[...], NN)
    width = out_ref.shape[1]
    r = lax.broadcasted_iota(jnp.int32, (LEAD, width), 0)
    c = lax.broadcasted_iota(jnp.int32, (LEAD, width), 1)
    global_col = (c // PANEL * (X_SIZE * Y_SIZE) + col) * PANEL + lax.rem(c, PANEL)
    out_ref[...] = jnp.where(global_col >= r, top, 0.0)

    for p in range(2):
        for off in range(1, N_ROW):
            rs_copy(p, off).wait_send()
            ag_copy(p, off).wait_send()
    for off in range(1, N_Z):
        crs_copy(off).wait_send()
        cag_copy(off).wait_send()

    def drain(k, carry):
        for tree in range(2):
            for panel in range(2):
                cond = sends(tree, panel)
                for way in range(4):
                    @pl.when(cond[way])
                    def _():
                        hop(k, tree, panel, way, False).wait_send()
        return carry

    lax.fori_loop(0, CHUNKS, drain, 0)


def local(panels):
    rows, width = panels.shape
    f32 = jnp.float32
    vmem, dma = pltpu.VMEM, pltpu.SemaphoreType.DMA
    return pl.pallas_call(
        kernel,
        out_shape=jax.ShapeDtypeStruct((LEAD, width), f32),
        in_specs=[pl.BlockSpec(memory_space=vmem)],
        out_specs=pl.BlockSpec(memory_space=vmem),
        scratch_shapes=[
            vmem((2, rows, PANEL), f32),
            vmem((2, LEAD, LEAD), f32),
            vmem((2, N_ROW - 1, N_ROW, LEAD), f32),
            vmem((2, LEAD, LEAD), f32),
            vmem((2, LEAD, LEAD), f32),
            vmem((LEAD, width), f32),
            vmem((PANEL, width), f32),
            vmem((PANEL, width), f32),
            vmem((N_Z - 1, LEAD // 2 // N_Z, width), f32),
            vmem((LEAD, width), f32),
            dma((CHUNKS * 4, 4)), dma((CHUNKS * 4,)),
            dma((2, N_ROW - 1)), dma((2, N_ROW - 1)),
            dma((2, N_ROW - 1)), dma((2, N_ROW - 1)),
            dma((2,)), dma((2,)),
            dma((N_Z - 1,)), dma((N_Z - 1,)),
            dma((N_Z - 1,)), dma((N_Z - 1,)),
        ],
        compiler_params=pltpu.CompilerParams(collective_id=0, has_side_effects=True),
    )(panels)


def solution(mesh):
    return jax.shard_map(local, mesh=mesh, in_specs=(P("row", "col"),), out_specs=P(None, "col"), check_vma=False)
```

```python
import jax
import jax.numpy as jnp
from jax import lax
from jax.experimental import pallas as pl
from jax.experimental.pallas import tpu as pltpu
from jax.sharding import PartitionSpec as P

PANEL = 128
LEAD = 2 * PANEL
LEAF = 64
GRAM = 3 * PANEL
X_SIZE = 4
Y_SIZE = 8
N_ROW = 16
N_Z = 8
CHUNKS = 1
MESH = pl.DeviceIdType.MESH
SUB = 8
HI = lax.Precision.HIGHEST


def dot(left, right, dims):
    return lax.dot_general(left, right, (dims, ((), ())), precision=HI, preferred_element_type=jnp.float32)


NN = ((1,), (0,))
NT = ((1,), (1,))
TN = ((0,), (0,))


def leaf_inverse(block):
    groups = LEAF // SUB
    sub = lax.broadcasted_iota(jnp.int32, (SUB, 128), 0)

    def step(g, rows):
        rows = list(rows)
        live = [None] + [(q < groups - g) for q in range(1, groups)]
        cols = [[jnp.broadcast_to(rows[q][:, i:i + 1], (SUB, 128)) for i in range(SUB)] for q in range(groups)]
        pivots = jnp.ones((SUB, 128), jnp.float32)
        for i in range(SUB):
            pivots = jnp.where(sub == i, cols[0][i], pivots)
            inv = 1.0 / jnp.broadcast_to(cols[0][i][i:i + 1], (SUB, 128))
            line = jnp.broadcast_to(rows[0][i:i + 1], (SUB, 128)) * inv
            heads = [None] * SUB
            for j in range(i + 1, SUB):
                heads[j] = jnp.broadcast_to(cols[0][j][i:i + 1], (SUB, 128)) * inv
            for q in range(groups):
                keep = sub > i if q == 0 else live[q]
                mult = jnp.where(keep, cols[q][i], 0.0)
                rows[q] = rows[q] - mult * line
                for j in range(i + 1, SUB):
                    cols[q][j] = cols[q][j] - mult * heads[j]
        scale = lax.rsqrt(pivots)
        scale = scale * (1.5 - 0.5 * pivots * scale * scale)
        rows[0] = rows[0] * scale
        rows = rows[1:] + rows[:1]
        return tuple(pltpu.roll(r, 128 - SUB, 1) for r in rows)

    rows = tuple(block[q * SUB:(q + 1) * SUB] for q in range(groups))
    rows = lax.fori_loop(0, groups, step, rows)
    rows = jnp.concatenate(rows, axis=0)
    return jnp.where(lax.broadcasted_iota(jnp.int32, rows.shape, 1) < LEAF, rows, 0.0)


def panel_inverse(block):
    r = lax.broadcasted_iota(jnp.int32, (LEAF, PANEL), 0)
    c = lax.broadcasted_iota(jnp.int32, (LEAF, PANEL), 1)
    unit = jnp.where(c == r + LEAF, 1.0, 0.0).astype(jnp.float32)
    none = jnp.zeros((LEAF, PANEL), jnp.float32)
    first = leaf_inverse(jnp.where(c < LEAF, block[:LEAF], unit))
    above = jnp.concatenate([first, none], axis=0)
    low = dot(block[LEAF:], above, NT)
    schur = block[LEAF:] - dot(low, jnp.concatenate([none, low], axis=0), NT)
    rest = unit - dot(low, above, NN)
    second = leaf_inverse(jnp.where(c < LEAF, pltpu.roll(schur, LEAF, 1), unit))
    return jnp.concatenate([first, dot(second, jnp.concatenate([rest, none], axis=0), NN)], axis=0)


def chol_inverse(gram_ref, inv_ref, between=lambda: None):
    first = panel_inverse(gram_ref[:PANEL])
    low = dot(gram_ref[PANEL:2 * PANEL], first, NT)
    schur = gram_ref[2 * PANEL:] - dot(low, low, NT)
    inv_ref[:PANEL, :PANEL] = first
    inv_ref[:PANEL, PANEL:] = jnp.zeros((PANEL, PANEL), jnp.float32)
    between()
    rest = dot(low, first, NN)
    second = panel_inverse(schur)
    inv_ref[PANEL:, PANEL:] = second
    inv_ref[PANEL:, :PANEL] = -dot(second, rest, NN)


def far_first(count):
    return sorted(range(1, count), key=lambda off: -min(off, count - off))


def kernel(panels_ref, out_ref, lead_ref, part_ref, recv_ref, gram_ref, inv_ref,
           c_part, c_pair, c_half, c_recv, cross_ref,
           bc_send, bc_recv, rs_send, rs_recv, ag_send, ag_recv,
           pair_send, pair_recv, crs_send, crs_recv, cag_send, cag_recv):
    me = lax.axis_index("row")
    col = lax.axis_index("col")
    core = lax.rem(me, 2)
    z = me // 2
    x = col // Y_SIZE
    y = lax.rem(col, Y_SIZE)

    def at_xy(dx, dy):
        return {"col": lax.rem(x + dx + X_SIZE, X_SIZE) * Y_SIZE + lax.rem(y + dy + Y_SIZE, Y_SIZE)}

    def row_peer(off):
        return {"row": lax.rem(me + off, N_ROW)}

    partner = {"row": z * 2 + 1 - core}
    near = [at_xy(0, 1), at_xy(0, -1), at_xy(1, 0), at_xy(-1, 0)]

    barrier = pltpu.get_barrier_semaphore()
    for off in far_first(N_ROW):
        pl.semaphore_signal(barrier, inc=1, device_id=row_peer(off), device_id_type=MESH)
    for device in near:
        pl.semaphore_signal(barrier, inc=1, device_id=device, device_id_type=MESH)
    pl.semaphore_wait(barrier, N_ROW - 1 + len(near))

    half_rows = lead_ref.shape[1] // 2
    size = half_rows // CHUNKS

    def sends(tree, panel):
        d = lax.rem(y - panel + Y_SIZE, Y_SIZE)
        up, down = d <= 3, (d == 0) | (d >= 6)
        if tree == 0:
            return [(x == 0) & up, (x == 0) & down, x <= 1, x == 0]
        return [(x != 0) & up, (x != 0) & down, (d == 0) & (x <= 1),
                ((d == 0) & (x == 0)) | ((d != 0) & (x == 1))]

    def relays(cond):
        return cond[0] | cond[1] | cond[2] | cond[3]

    def hop(k, tree, panel, way, own):
        rows = pl.ds(pl.multiple_of(tree * half_rows + k * size, size), size)
        piece = (k * 2 + tree) * 2 + panel
        return pltpu.make_async_remote_copy(
            src_ref=panels_ref.at[rows, pl.ds(0, PANEL)] if own else lead_ref.at[panel, rows],
            dst_ref=lead_ref.at[panel, rows],
            send_sem=bc_send.at[piece, way], recv_sem=bc_recv.at[piece],
            device_id=near[way], device_id_type=MESH)

    def send_own(k, carry):
        for panel in range(2):
            @pl.when(col == panel)
            def _():
                for tree in range(2):
                    cond = sends(tree, panel)
                    for way in range(4):
                        @pl.when(cond[way])
                        def _():
                            hop(k, tree, panel, way, True).start()
        return carry

    def pass_on(k, carry):
        for tree in range(2):
            for panel in range(2):
                cond = sends(tree, panel)

                @pl.when((col != panel) & relays(cond))
                def _():
                    hop(k, tree, panel, 0, False).wait_recv()
                    for way in range(4):
                        @pl.when(cond[way])
                        def _():
                            hop(k, tree, panel, way, False).start()
        return carry

    def take_last(k, carry):
        for tree in range(2):
            for panel in range(2):
                @pl.when((col != panel) & jnp.logical_not(relays(sends(tree, panel))))
                def _():
                    hop(k, tree, panel, 0, False).wait_recv()
        return carry

    lax.fori_loop(0, CHUNKS, send_own, 0)
    lax.fori_loop(0, CHUNKS, pass_on, 0)
    lax.fori_loop(0, CHUNKS, take_last, 0)
    for panel in range(2):
        @pl.when(col == panel)
        def _():
            lead_ref[panel] = panels_ref[:, :PANEL]

    def lead():
        return jnp.concatenate([lead_ref[0], lead_ref[1]], axis=1)

    own_rows = GRAM // N_ROW
    mine = pl.ds(pl.multiple_of(me * own_rows, own_rows), own_rows)

    def rs_copy(p, off):
        peer = lax.rem(me + off, N_ROW)
        return pltpu.make_async_remote_copy(
            src_ref=part_ref.at[p, pl.ds(pl.multiple_of(peer * own_rows, own_rows), own_rows)],
            dst_ref=recv_ref.at[p, off - 1],
            send_sem=rs_send.at[p, off - 1], recv_sem=rs_recv.at[p, off - 1],
            device_id=row_peer(off), device_id_type=MESH)

    def ag_copy(p, off):
        return pltpu.make_async_remote_copy(
            src_ref=gram_ref.at[p, mine], dst_ref=gram_ref.at[p, mine],
            send_sem=ag_send.at[p, off - 1], recv_sem=ag_recv.at[p, off - 1],
            device_id=row_peer(off), device_id_type=MESH)

    def gram_blocks(p, left, right, dims):
        part_ref[p, :PANEL] = dot(left, left, dims)
        part_ref[p, PANEL:2 * PANEL] = dot(right, left, dims)
        part_ref[p, 2 * PANEL:] = dot(right, right, dims)

    def scatter_start(p):
        for off in far_first(N_ROW):
            rs_copy(p, off).start()

    def scatter_finish(p):
        total = part_ref[p, mine]
        for off in reversed(far_first(N_ROW)):
            rs_copy(p, off).wait_recv()
            total = total + recv_ref[p, off - 1]
        gram_ref[p, mine] = total
        for off in far_first(N_ROW):
            ag_copy(p, off).start()

    def gather_finish(p):
        for off in reversed(far_first(N_ROW)):
            ag_copy(p, off).wait_recv()

    c_rows = LEAD // 2 // N_Z
    keep = pl.ds(pl.multiple_of(core * PANEL, PANEL), PANEL)
    give = pl.ds(pl.multiple_of((1 - core) * PANEL, PANEL), PANEL)
    c_mine = pl.ds(pl.multiple_of(core * PANEL + z * c_rows, c_rows), c_rows)

    def pair_copy(step):
        return pltpu.make_async_remote_copy(
            src_ref=cross_ref.at[keep] if step else c_part.at[give],
            dst_ref=cross_ref.at[keep] if step else c_pair,
            send_sem=pair_send.at[step], recv_sem=pair_recv.at[step],
            device_id=partner, device_id_type=MESH)

    def crs_copy(off):
        peer_z = lax.rem(z + off, N_Z)
        return pltpu.make_async_remote_copy(
            src_ref=c_half.at[pl.ds(pl.multiple_of(peer_z * c_rows, c_rows), c_rows)],
            dst_ref=c_recv.at[off - 1],
            send_sem=crs_send.at[off - 1], recv_sem=crs_recv.at[off - 1],
            device_id=row_peer(2 * off), device_id_type=MESH)

    def cag_copy(off):
        return pltpu.make_async_remote_copy(
            src_ref=cross_ref.at[c_mine], dst_ref=cross_ref.at[c_mine],
            send_sem=cag_send.at[off - 1], recv_sem=cag_recv.at[off - 1],
            device_id=row_peer(2 * off), device_id_type=MESH)

    def cross_scatter():
        pair_copy(0).wait_recv()
        c_half[...] = c_part[keep] + c_pair[...]
        for off in far_first(N_Z):
            crs_copy(off).start()

    def cross_gather():
        total = c_half[pl.ds(pl.multiple_of(z * c_rows, c_rows), c_rows)]
        for off in reversed(far_first(N_Z)):
            crs_copy(off).wait_recv()
            total = total + c_recv[off - 1]
        cross_ref[c_mine] = total
        for off in far_first(N_Z):
            cag_copy(off).start()

    def cross_pair():
        for off in far_first(N_Z):
            cag_copy(off).wait_recv()
        pair_copy(1).start()

    gram_blocks(0, lead_ref[0], lead_ref[1], TN)
    scatter_start(0)
    c_part[...] = dot(lead(), panels_ref[...], TN)
    pair_copy(0).start()
    scatter_finish(0)
    gather_finish(0)
    cross_scatter()
    chol_inverse(gram_ref.at[0], inv_ref.at[0], cross_gather)
    basis = dot(inv_ref[0], lead(), NT)
    gram_blocks(1, basis[:PANEL], basis[PANEL:], NT)
    scatter_start(1)
    cross_pair()
    scatter_finish(1)
    pair_copy(1).wait_recv()
    c_part_done = [pair_copy(0), pair_copy(1)]
    for copy in c_part_done:
        copy.wait_send()
    c_part[...] = dot(inv_ref[0], cross_ref[...], NN)
    gather_finish(1)
    chol_inverse(gram_ref.at[1], inv_ref.at[1])
    top = dot(inv_ref[1], c_part[...], NN)
    width = out_ref.shape[1]
    r = lax.broadcasted_iota(jnp.int32, (LEAD, width), 0)
    c = lax.broadcasted_iota(jnp.int32, (LEAD, width), 1)
    global_col = (c // PANEL * (X_SIZE * Y_SIZE) + col) * PANEL + lax.rem(c, PANEL)
    out_ref[...] = jnp.where(global_col >= r, top, 0.0)

    for p in range(2):
        for off in range(1, N_ROW):
            rs_copy(p, off).wait_send()
            ag_copy(p, off).wait_send()
    for off in range(1, N_Z):
        crs_copy(off).wait_send()
        cag_copy(off).wait_send()

    def drain(k, carry):
        for tree in range(2):
            for panel in range(2):
                cond = sends(tree, panel)
                for way in range(4):
                    @pl.when(cond[way])
                    def _():
                        hop(k, tree, panel, way, False).wait_send()
        return carry

    lax.fori_loop(0, CHUNKS, drain, 0)


def local(panels):
    rows, width = panels.shape
    f32 = jnp.float32
    vmem, dma = pltpu.VMEM, pltpu.SemaphoreType.DMA
    return pl.pallas_call(
        kernel,
        out_shape=jax.ShapeDtypeStruct((LEAD, width), f32),
        in_specs=[pl.BlockSpec(memory_space=vmem)],
        out_specs=pl.BlockSpec(memory_space=vmem),
        scratch_shapes=[
            vmem((2, rows, PANEL), f32),
            vmem((2, GRAM, PANEL), f32),
            vmem((2, N_ROW - 1, GRAM // N_ROW, PANEL), f32),
            vmem((2, GRAM, PANEL), f32),
            vmem((2, LEAD, LEAD), f32),
            vmem((LEAD, width), f32),
            vmem((PANEL, width), f32),
            vmem((PANEL, width), f32),
            vmem((N_Z - 1, LEAD // 2 // N_Z, width), f32),
            vmem((LEAD, width), f32),
            dma((CHUNKS * 4, 4)), dma((CHUNKS * 4,)),
            dma((2, N_ROW - 1)), dma((2, N_ROW - 1)),
            dma((2, N_ROW - 1)), dma((2, N_ROW - 1)),
            dma((2,)), dma((2,)),
            dma((N_Z - 1,)), dma((N_Z - 1,)),
            dma((N_Z - 1,)), dma((N_Z - 1,)),
        ],
        compiler_params=pltpu.CompilerParams(collective_id=0, has_side_effects=True),
    )(panels)


def solution(mesh):
    return jax.shard_map(local, mesh=mesh, in_specs=(P("row", "col"),), out_specs=P(None, "col"), check_vma=False)
```

```python
import jax
import jax.numpy as jnp
from jax import lax
from jax.experimental import pallas as pl
from jax.experimental.pallas import tpu as pltpu
from jax.sharding import PartitionSpec as P

PANEL = 128
LEAD = 2 * PANEL
LEAF = 64
GRAM = 3 * PANEL
X_SIZE = 4
Y_SIZE = 8
N_ROW = 16
N_Z = 8
CHUNKS = 1
MESH = pl.DeviceIdType.MESH
SUB = 8
HI = lax.Precision.HIGHEST


def dot(left, right, dims):
    return lax.dot_general(left, right, (dims, ((), ())), precision=HI, preferred_element_type=jnp.float32)


NN = ((1,), (0,))
NT = ((1,), (1,))
TN = ((0,), (0,))


def leaf_inverse(block):
    groups = LEAF // SUB
    sub = lax.broadcasted_iota(jnp.int32, (SUB, 128), 0)

    def step(g, rows):
        rows = list(rows)
        live = [None] + [(q < groups - g) for q in range(1, groups)]
        cols = [[jnp.broadcast_to(rows[q][:, i:i + 1], (SUB, 128)) for i in range(SUB)] for q in range(groups)]
        pivots = jnp.ones((SUB, 128), jnp.float32)
        for i in range(SUB):
            pivots = jnp.where(sub == i, cols[0][i], pivots)
            inv = 1.0 / jnp.broadcast_to(cols[0][i][i:i + 1], (SUB, 128))
            line = jnp.broadcast_to(rows[0][i:i + 1], (SUB, 128)) * inv
            heads = [None] * SUB
            for j in range(i + 1, SUB):
                heads[j] = jnp.broadcast_to(cols[0][j][i:i + 1], (SUB, 128)) * inv
            for q in range(groups):
                keep = sub > i if q == 0 else live[q]
                mult = jnp.where(keep, cols[q][i], 0.0)
                rows[q] = rows[q] - mult * line
                for j in range(i + 1, SUB):
                    cols[q][j] = cols[q][j] - mult * heads[j]
        scale = lax.rsqrt(pivots)
        scale = scale * (1.5 - 0.5 * pivots * scale * scale)
        rows[0] = rows[0] * scale
        rows = rows[1:] + rows[:1]
        return tuple(pltpu.roll(r, 128 - SUB, 1) for r in rows)

    rows = tuple(block[q * SUB:(q + 1) * SUB] for q in range(groups))
    rows = lax.fori_loop(0, groups, step, rows)
    rows = jnp.concatenate(rows, axis=0)
    return jnp.where(lax.broadcasted_iota(jnp.int32, rows.shape, 1) < LEAF, rows, 0.0)


def panel_inverse(block):
    r = lax.broadcasted_iota(jnp.int32, (LEAF, PANEL), 0)
    c = lax.broadcasted_iota(jnp.int32, (LEAF, PANEL), 1)
    unit = jnp.where(c == r + LEAF, 1.0, 0.0).astype(jnp.float32)
    none = jnp.zeros((LEAF, PANEL), jnp.float32)
    first = leaf_inverse(jnp.where(c < LEAF, block[:LEAF], unit))
    above = jnp.concatenate([first, none], axis=0)
    low = dot(block[LEAF:], above, NT)
    schur = block[LEAF:] - dot(low, jnp.concatenate([none, low], axis=0), NT)
    rest = unit - dot(low, above, NN)
    second = leaf_inverse(jnp.where(c < LEAF, pltpu.roll(schur, LEAF, 1), unit))
    return jnp.concatenate([first, dot(second, jnp.concatenate([rest, none], axis=0), NN)], axis=0)


def chol_inverse(gram_ref, inv_ref, between=lambda: None):
    first = panel_inverse(gram_ref[:PANEL])
    low = dot(gram_ref[PANEL:2 * PANEL], first, NT)
    schur = gram_ref[2 * PANEL:] - dot(low, low, NT)
    inv_ref[:PANEL, :PANEL] = first
    inv_ref[:PANEL, PANEL:] = jnp.zeros((PANEL, PANEL), jnp.float32)
    between()
    rest = dot(low, first, NN)
    second = panel_inverse(schur)
    inv_ref[PANEL:, PANEL:] = second
    inv_ref[PANEL:, :PANEL] = -dot(second, rest, NN)


def far_first(count):
    return sorted(range(1, count), key=lambda off: -min(off, count - off))


def kernel(panels_ref, out_ref, lead_ref, part_ref, recv_ref, gram_ref, inv_ref,
           c_part, c_pair, c_half, c_recv, cross_ref,
           bc_send, bc_recv, rs_send, rs_recv, ag_send, ag_recv,
           pair_send, pair_recv, crs_send, crs_recv, cag_send, cag_recv):
    me = lax.axis_index("row")
    col = lax.axis_index("col")
    core = lax.rem(me, 2)
    z = me // 2
    x = col // Y_SIZE
    y = lax.rem(col, Y_SIZE)

    def at_xy(dx, dy):
        return {"col": lax.rem(x + dx + X_SIZE, X_SIZE) * Y_SIZE + lax.rem(y + dy + Y_SIZE, Y_SIZE)}

    def row_peer(off):
        return {"row": lax.rem(me + off, N_ROW)}

    partner = {"row": z * 2 + 1 - core}
    near = [at_xy(0, 1), at_xy(0, -1), at_xy(1, 0), at_xy(-1, 0), at_xy(2, 0)]

    barrier = pltpu.get_barrier_semaphore()
    for off in far_first(N_ROW):
        pl.semaphore_signal(barrier, inc=1, device_id=row_peer(off), device_id_type=MESH)
    for device in near:
        pl.semaphore_signal(barrier, inc=1, device_id=device, device_id_type=MESH)
    pl.semaphore_wait(barrier, N_ROW - 1 + len(near))

    half_rows = lead_ref.shape[1] // 2
    size = half_rows // CHUNKS

    def sends(tree, panel):
        d = lax.rem(y - panel + Y_SIZE, Y_SIZE)
        up, down = d <= 3, (d == 0) | (d >= 6)
        if tree == 0:
            return [(x == 0) & up, (x == 0) & down, x == 0, x == 0, x == 0]
        return [(x != 0) & up, (x != 0) & down, (d == 0) & (x == 0),
                ((d == 0) & (x == 0)) | ((d != 0) & (x == 1)), (d == 0) & (x == 0)]

    def relays(cond):
        return cond[0] | cond[1] | cond[2] | cond[3] | cond[4]

    def hop(k, tree, panel, way, own):
        rows = pl.ds(pl.multiple_of(tree * half_rows + k * size, size), size)
        piece = (k * 2 + tree) * 2 + panel
        return pltpu.make_async_remote_copy(
            src_ref=panels_ref.at[rows, pl.ds(0, PANEL)] if own else lead_ref.at[panel, rows],
            dst_ref=lead_ref.at[panel, rows],
            send_sem=bc_send.at[piece, way], recv_sem=bc_recv.at[piece],
            device_id=near[way], device_id_type=MESH)

    def send_own(k, carry):
        for panel in range(2):
            @pl.when(col == panel)
            def _():
                for tree in range(2):
                    cond = sends(tree, panel)
                    for way in range(5):
                        @pl.when(cond[way])
                        def _():
                            hop(k, tree, panel, way, True).start()
        return carry

    def pass_on(k, carry):
        for tree in range(2):
            for panel in range(2):
                cond = sends(tree, panel)

                @pl.when((col != panel) & relays(cond))
                def _():
                    hop(k, tree, panel, 0, False).wait_recv()
                    for way in range(5):
                        @pl.when(cond[way])
                        def _():
                            hop(k, tree, panel, way, False).start()
        return carry

    def take_last(k, carry):
        for tree in range(2):
            for panel in range(2):
                @pl.when((col != panel) & jnp.logical_not(relays(sends(tree, panel))))
                def _():
                    hop(k, tree, panel, 0, False).wait_recv()
        return carry

    lax.fori_loop(0, CHUNKS, send_own, 0)
    lax.fori_loop(0, CHUNKS, pass_on, 0)
    lax.fori_loop(0, CHUNKS, take_last, 0)
    for panel in range(2):
        @pl.when(col == panel)
        def _():
            lead_ref[panel] = panels_ref[:, :PANEL]

    def lead():
        return jnp.concatenate([lead_ref[0], lead_ref[1]], axis=1)

    own_rows = GRAM // N_ROW
    mine = pl.ds(pl.multiple_of(me * own_rows, own_rows), own_rows)

    def rs_copy(p, off):
        peer = lax.rem(me + off, N_ROW)
        return pltpu.make_async_remote_copy(
            src_ref=part_ref.at[p, pl.ds(pl.multiple_of(peer * own_rows, own_rows), own_rows)],
            dst_ref=recv_ref.at[p, off - 1],
            send_sem=rs_send.at[p, off - 1], recv_sem=rs_recv.at[p, off - 1],
            device_id=row_peer(off), device_id_type=MESH)

    def ag_copy(p, off):
        return pltpu.make_async_remote_copy(
            src_ref=gram_ref.at[p, mine], dst_ref=gram_ref.at[p, mine],
            send_sem=ag_send.at[p, off - 1], recv_sem=ag_recv.at[p, off - 1],
            device_id=row_peer(off), device_id_type=MESH)

    def gram_blocks(p, left, right, dims):
        part_ref[p, :PANEL] = dot(left, left, dims)
        part_ref[p, PANEL:2 * PANEL] = dot(right, left, dims)
        part_ref[p, 2 * PANEL:] = dot(right, right, dims)

    def scatter_start(p):
        for off in far_first(N_ROW):
            rs_copy(p, off).start()

    def scatter_finish(p):
        total = part_ref[p, mine]
        for off in reversed(far_first(N_ROW)):
            rs_copy(p, off).wait_recv()
            total = total + recv_ref[p, off - 1]
        gram_ref[p, mine] = total
        for off in far_first(N_ROW):
            ag_copy(p, off).start()

    def gather_finish(p):
        for off in reversed(far_first(N_ROW)):
            ag_copy(p, off).wait_recv()

    c_rows = LEAD // 2 // N_Z
    keep = pl.ds(pl.multiple_of(core * PANEL, PANEL), PANEL)
    give = pl.ds(pl.multiple_of((1 - core) * PANEL, PANEL), PANEL)
    c_mine = pl.ds(pl.multiple_of(core * PANEL + z * c_rows, c_rows), c_rows)

    def pair_copy(step):
        return pltpu.make_async_remote_copy(
            src_ref=cross_ref.at[keep] if step else c_part.at[give],
            dst_ref=cross_ref.at[keep] if step else c_pair,
            send_sem=pair_send.at[step], recv_sem=pair_recv.at[step],
            device_id=partner, device_id_type=MESH)

    def crs_copy(off):
        peer_z = lax.rem(z + off, N_Z)
        return pltpu.make_async_remote_copy(
            src_ref=c_half.at[pl.ds(pl.multiple_of(peer_z * c_rows, c_rows), c_rows)],
            dst_ref=c_recv.at[off - 1],
            send_sem=crs_send.at[off - 1], recv_sem=crs_recv.at[off - 1],
            device_id=row_peer(2 * off), device_id_type=MESH)

    def cag_copy(off):
        return pltpu.make_async_remote_copy(
            src_ref=cross_ref.at[c_mine], dst_ref=cross_ref.at[c_mine],
            send_sem=cag_send.at[off - 1], recv_sem=cag_recv.at[off - 1],
            device_id=row_peer(2 * off), device_id_type=MESH)

    def cross_scatter():
        pair_copy(0).wait_recv()
        c_half[...] = c_part[keep] + c_pair[...]
        for off in far_first(N_Z):
            crs_copy(off).start()

    def cross_gather():
        total = c_half[pl.ds(pl.multiple_of(z * c_rows, c_rows), c_rows)]
        for off in reversed(far_first(N_Z)):
            crs_copy(off).wait_recv()
            total = total + c_recv[off - 1]
        cross_ref[c_mine] = total
        for off in far_first(N_Z):
            cag_copy(off).start()

    def cross_pair():
        for off in far_first(N_Z):
            cag_copy(off).wait_recv()
        pair_copy(1).start()

    gram_blocks(0, lead_ref[0], lead_ref[1], TN)
    scatter_start(0)
    c_part[...] = dot(lead(), panels_ref[...], TN)
    pair_copy(0).start()
    scatter_finish(0)
    gather_finish(0)
    cross_scatter()
    chol_inverse(gram_ref.at[0], inv_ref.at[0], cross_gather)
    basis = dot(inv_ref[0], lead(), NT)
    gram_blocks(1, basis[:PANEL], basis[PANEL:], NT)
    scatter_start(1)
    cross_pair()
    scatter_finish(1)
    pair_copy(1).wait_recv()
    c_part_done = [pair_copy(0), pair_copy(1)]
    for copy in c_part_done:
        copy.wait_send()
    c_part[...] = dot(inv_ref[0], cross_ref[...], NN)
    gather_finish(1)
    chol_inverse(gram_ref.at[1], inv_ref.at[1])
    top = dot(inv_ref[1], c_part[...], NN)
    width = out_ref.shape[1]
    r = lax.broadcasted_iota(jnp.int32, (LEAD, width), 0)
    c = lax.broadcasted_iota(jnp.int32, (LEAD, width), 1)
    global_col = (c // PANEL * (X_SIZE * Y_SIZE) + col) * PANEL + lax.rem(c, PANEL)
    out_ref[...] = jnp.where(global_col >= r, top, 0.0)

    for p in range(2):
        for off in range(1, N_ROW):
            rs_copy(p, off).wait_send()
            ag_copy(p, off).wait_send()
    for off in range(1, N_Z):
        crs_copy(off).wait_send()
        cag_copy(off).wait_send()

    def drain(k, carry):
        for tree in range(2):
            for panel in range(2):
                cond = sends(tree, panel)
                for way in range(5):
                    @pl.when(cond[way])
                    def _():
                        hop(k, tree, panel, way, False).wait_send()
        return carry

    lax.fori_loop(0, CHUNKS, drain, 0)


def local(panels):
    rows, width = panels.shape
    f32 = jnp.float32
    vmem, dma = pltpu.VMEM, pltpu.SemaphoreType.DMA
    return pl.pallas_call(
        kernel,
        out_shape=jax.ShapeDtypeStruct((LEAD, width), f32),
        in_specs=[pl.BlockSpec(memory_space=vmem)],
        out_specs=pl.BlockSpec(memory_space=vmem),
        scratch_shapes=[
            vmem((2, rows, PANEL), f32),
            vmem((2, GRAM, PANEL), f32),
            vmem((2, N_ROW - 1, GRAM // N_ROW, PANEL), f32),
            vmem((2, GRAM, PANEL), f32),
            vmem((2, LEAD, LEAD), f32),
            vmem((LEAD, width), f32),
            vmem((PANEL, width), f32),
            vmem((PANEL, width), f32),
            vmem((N_Z - 1, LEAD // 2 // N_Z, width), f32),
            vmem((LEAD, width), f32),
            dma((CHUNKS * 4, 5)), dma((CHUNKS * 4,)),
            dma((2, N_ROW - 1)), dma((2, N_ROW - 1)),
            dma((2, N_ROW - 1)), dma((2, N_ROW - 1)),
            dma((2,)), dma((2,)),
            dma((N_Z - 1,)), dma((N_Z - 1,)),
            dma((N_Z - 1,)), dma((N_Z - 1,)),
        ],
        compiler_params=pltpu.CompilerParams(collective_id=0, has_side_effects=True),
    )(panels)


def solution(mesh):
    return jax.shard_map(local, mesh=mesh, in_specs=(P("row", "col"),), out_specs=P(None, "col"), check_vma=False)
```
